512 devices in a mesh: dp: 32 (over x, z), hidden: 16 (over y, core).
Axes of the slice: x: 4, y: 8, z: 8, core: 2. Of those that a mesh axis runs over, the one named last changes fastest.
Arguments:
- activations: bfloat16 [4096, 768], P(('dp', 'hidden')), may hold values from -6 to 6
- grad_out: bfloat16 [4096, 53248], P('dp', 'hidden'), may hold values from -8 to 8
- momentum: float32 [768, 53248], P('dp', 'hidden'), may hold values from -6 to 6
Outputs:
- new_momentum: float32 [768, 53248], P('dp', 'hidden')
The draws below stay inside these ranges and needn't reach their ends.
All inputs are finite; a program needn't handle non-finite values.
Results may differ from the reference program's by a relative error of at most 0.0003.
Values may be sent and summed in bfloat16 or wider, within the bound.
No kernel may reach another device: no remote copies, remote signals or barrier semaphores. Data moves between devices by JAX's collectives and lax.ppermute only.
A program may use at most 64 MiB of HBM per device.

```python
import jax
import jax.numpy as jnp
from jax import lax

FF = 53248
DWIN = 768
TOK = 128
TOKENS = 4096
REPLICAS = 32
LEVELS = 5
N_DP = 32
N_HIDDEN = 16


def draw_activations(key, part):
    common_key = jax.random.fold_in(key, 11)
    private_key = jax.random.fold_in(key, 12)
    common = jnp.clip(jax.random.normal(common_key, (TOK, DWIN), jnp.float32), -4.0, 4.0)
    private = jnp.clip(jax.random.normal(private_key, (REPLICAS, TOK, DWIN), jnp.float32), -4.0, 4.0)
    blended = 0.8 * common[None] + 0.6 * private
    return blended.reshape(TOKENS, DWIN).astype(jnp.bfloat16)


def draw_grad_out(key, part):
    common_key = jax.random.fold_in(key, 21)
    share_key = jax.random.fold_in(key, 22)
    common = jnp.clip(jax.random.normal(common_key, (TOK, FF), jnp.float32), -5.0, 5.0)
    shares = jax.random.uniform(share_key, (REPLICAS,), jnp.float32, 0.3, 0.9)
    column_scale = jnp.exp(jnp.log(10.0) * jax.random.uniform(jax.random.fold_in(key, 23), (FF,), jnp.float32))
    column_scale = column_scale * 3.0 ** (jnp.arange(FF, dtype=jnp.float32) / max(FF - 1, 1))
    replica_scale = 3.0 ** (jnp.arange(REPLICAS, dtype=jnp.float32) / max(REPLICAS - 1, 1))
    norm_factor = 1.0 / (5.0 * (TOK * REPLICAS) ** 0.5)
    private_base = jax.random.fold_in(key, 24)

    def one_replica(replica):
        private_key = jax.random.fold_in(private_base, replica)
        private = jnp.clip(jax.random.normal(private_key, (TOK, FF), jnp.float32), -5.0, 5.0)
        share = shares[replica]
        blended = share * common + jnp.sqrt(1.0 - share * share) * private
        return (blended * column_scale * (replica_scale[replica] * norm_factor)).astype(jnp.bfloat16)
    stacked = lax.map(one_replica, jnp.arange(REPLICAS, dtype=jnp.int32))
    return stacked.reshape(TOKENS, FF)


def block_scale(rng, shape, pieces, smallest, largest):
    level, own = 1.0, jax.random.fold_in(rng, 6)
    for axis_at, shards_of in pieces:
        heights = jnp.exp(jax.random.uniform(jax.random.fold_in(own, axis_at), (shards_of,), jnp.float32, smallest / len(pieces), largest / len(pieces)))
        level = level * jnp.repeat(heights, shape[axis_at] // shards_of).reshape([-1 if axis == axis_at else 1 for axis in range(len(shape))])
    return level


def bell_draw(rng, dims, spread, limit, split=(), kind=jnp.bfloat16):
    drawn = spread * jax.random.normal(rng, dims, jnp.float32)
    if split:
        drawn = drawn * block_scale(rng, dims, split, -0.22, 0.18)
    return jnp.clip(drawn, -limit, limit).astype(kind)


def setup_inputs(seed: int = 0) -> dict:
    arg_keys = jax.random.split(jax.random.key(seed), 4)
    return {
        "activations": draw_activations(jax.random.fold_in(arg_keys[3], 71), 0),
        "grad_out": draw_grad_out(jax.random.fold_in(arg_keys[3], 71), 0),
        "momentum": bell_draw(arg_keys[2], (DWIN, FF), 1.0, 6.0, ((0, 32), (1, 16)), jnp.float32),
    }


EPSILON = 1e-6
DECAY = 0.9


def replica_grads(activations, grad_out, col_start, block_width):
    act_rows = activations.reshape(N_DP, TOK, DWIN).astype(jnp.float32)
    upstream = lax.dynamic_slice_in_dim(grad_out, col_start, block_width, 1)
    upstream = upstream.reshape(N_DP, TOK, block_width).astype(jnp.float32)
    return jnp.einsum('rtd,rtf->rdf', act_rows, upstream, precision=lax.Precision.HIGHEST)


def reference(activations, grad_out, momentum):
    block_width = FF // N_HIDDEN

    def gram_step(gram_matrix, block_id):
        gradients = replica_grads(activations, grad_out, (block_id * block_width).astype(jnp.int32), block_width)
        flattened = gradients.reshape(N_DP, DWIN * block_width)
        return gram_matrix + jnp.dot(flattened, flattened.T, precision=lax.Precision.HIGHEST), None

    gram_matrix, leftover = lax.scan(gram_step, jnp.zeros((N_DP, N_DP), jnp.float32), jnp.arange(N_HIDDEN, dtype=jnp.int32))
    coefficients = jnp.eye(N_DP, dtype=jnp.float32)
    for level_index in range(LEVELS):
        paired = coefficients.reshape(-1, 2, N_DP)
        lower_vec = paired[:, 0]
        upper_vec = paired[:, 1]
        lower_sq = jnp.einsum('ir,rs,is->i', lower_vec, gram_matrix, lower_vec, precision=lax.Precision.HIGHEST)
        upper_sq = jnp.einsum('ir,rs,is->i', upper_vec, gram_matrix, upper_vec, precision=lax.Precision.HIGHEST)
        cross = jnp.einsum('ir,rs,is->i', lower_vec, gram_matrix, upper_vec, precision=lax.Precision.HIGHEST)
        lower_coef = 1.0 - cross / (2.0 * (lower_sq + EPSILON))
        upper_coef = 1.0 - cross / (2.0 * (upper_sq + EPSILON))
        coefficients = lower_coef[:, None] * lower_vec + upper_coef[:, None] * upper_vec
    weights = coefficients[0]

    def output_step(unused, block_id):
        gradients = replica_grads(activations, grad_out, (block_id * block_width).astype(jnp.int32), block_width)
        return unused, jnp.einsum('r,rdf->df', weights, gradients, precision=lax.Precision.HIGHEST)

    leftover, blocks = lax.scan(output_step, jnp.zeros((), jnp.float32), jnp.arange(N_HIDDEN, dtype=jnp.int32))
    combined = blocks.transpose(1, 0, 2).reshape(DWIN, FF)
    return DECAY * momentum + combined
```

```python
import functools

import jax
import jax.numpy as jnp
from jax import lax
from jax.experimental import pallas as pl
from jax.experimental.pallas import tpu as pltpu
from jax.sharding import Mesh, PartitionSpec as P

EPSILON = 1e-06
DECAY = 0.9
NR = 32
TOK = 128
LANES = 128
XZ = ("x", "z")
CORES = [(0, 1), (1, 0)]


def gram_kernel(own_ref, oth_ref, a_ref, g_out_ref, gram_ref, g_ref, q_ref):
    r = pl.program_id(0)
    cols = own_ref.shape[1]
    depth = a_ref.shape[-1]
    act = a_ref[...].reshape(TOK, depth)
    for part, ref in enumerate((own_ref, oth_ref)):
        block = jnp.dot(ref[0], act, preferred_element_type=jnp.float32)
        g_ref[r, pl.ds(part * cols, cols), :] = block
        g_out_ref[0, pl.ds(part * cols, cols), :] = block

    @pl.when(r == NR - 1)
    def _():
        q_ref[...] = jnp.zeros_like(q_ref)
        groups = 2 * cols // 8
        lane_blocks = depth // LANES

        def pair_block(rb, sb):
            def body(f, acc):
                acc = list(acc)
                for half in range(2):
                    row = pl.multiple_of((f * 2 + half) * 8, 8)
                    for lb in range(lane_blocks):
                        lanes = slice(lb * LANES, (lb + 1) * LANES)
                        left = [g_ref[rb * 4 + i, pl.ds(row, 8), lanes] for i in range(4)]
                        right = [g_ref[sb * 4 + i, pl.ds(row, 8), lanes] for i in range(4)]
                        for i in range(4):
                            for j in range(4):
                                acc[i * 4 + j] = acc[i * 4 + j] + left[i] * right[j]
                return tuple(acc)

            zero = jnp.zeros((8, LANES), jnp.float32)
            acc = lax.fori_loop(0, groups // 2, body, (zero,) * 16)
            for i in range(4):
                left_id = rb * 4 + i
                base = lax.rem(left_id, 8) * 128 + lax.div(left_id, 8) * 32
                for j in range(4):
                    q_ref[pl.ds(base + sb * 4 + j, 1), :] = jnp.sum(
                        acc[i * 4 + j], axis=0, keepdims=True
                    )

        def outer(rb, carry):
            def inner(sb, c):
                pair_block(rb, sb)
                return c

            return lax.fori_loop(rb, NR // 4, inner, carry)

        lax.fori_loop(0, NR // 4, outer, 0)
        sums = lax.dot_general(
            jnp.ones((8, LANES), jnp.float32),
            q_ref[...],
            (((1,), (1,)), ((), ())),
            precision=lax.Precision.HIGHEST,
            preferred_element_type=jnp.float32,
        )
        for i in range(8):
            gram_ref[i : i + 1, :] = sums[i : i + 1, i * LANES : (i + 1) * LANES]


def tree_weights(packed):
    gram = jnp.concatenate([packed[:, 32 * q : 32 * q + 32] for q in range(4)], axis=0)
    rows = lax.broadcasted_iota(jnp.int32, (NR, NR), 0)
    cols = lax.broadcasted_iota(jnp.int32, (NR, NR), 1)
    upper = jnp.where(rows < cols, gram, 0.0)
    quad = jnp.where(rows == cols, gram, 2.0 * upper)
    w_col = jnp.ones((NR, 1), jnp.float32)
    w_row = jnp.ones((1, NR), jnp.float32)
    for level in range(5):
        scale = w_col * w_row
        same_half = (rows >> level) == (cols >> level)
        same_pair = (rows >> (level + 1)) == (cols >> (level + 1))
        squares = jnp.where(same_half, quad * scale, 0.0)
        crosses = jnp.where(same_pair & (~same_half), upper * scale, 0.0)

        def both(values, mask):
            down = jnp.sum(values, axis=1, keepdims=True)
            across = jnp.sum(values, axis=0, keepdims=True)
            as_row = jnp.sum(jnp.where(mask, down, 0.0), axis=0, keepdims=True)
            as_col = jnp.sum(jnp.where(mask, across, 0.0), axis=1, keepdims=True)
            return as_col, as_row

        sq_col, sq_row = both(squares, same_half)
        cr_col, cr_row = both(crosses, same_pair)
        w_col = w_col * (1.0 - cr_col / (2.0 * (sq_col + EPSILON)))
        w_row = w_row * (1.0 - cr_row / (2.0 * (sq_row + EPSILON)))
    return w_col


def combine_kernel(part_ref, g_ref, c_ref, w_ref, ct_ref):
    step = pl.program_id(0)
    block = g_ref.shape[1]
    depth = g_ref.shape[2]
    cols = (pl.num_programs(0) * block) // 2

    @pl.when(step == 0)
    def _():
        packed = part_ref[0]
        for k in range(1, part_ref.shape[0]):
            packed = packed + part_ref[k]
        w_ref[...] = jnp.broadcast_to(tree_weights(packed), (NR, LANES))
        ct_ref[pl.ds(ct_ref.shape[0] - 48, 48), :] = jnp.zeros((48, depth), jnp.float32)

    for lb in range(depth // LANES):
        lanes = slice(lb * LANES, (lb + 1) * LANES)
        acc = g_ref[0, :, lanes] * w_ref[0:1, :]
        for r in range(1, NR):
            acc = acc + g_ref[r, :, lanes] * w_ref[r : r + 1, :]
        ct_ref[pl.ds(pl.multiple_of(step * block, 8), block), lanes] = acc

    @pl.when(step == pl.num_programs(0) - 1)
    def _():
        for part in range(2):
            for lb in range(depth // LANES):
                lanes = slice(lb * LANES, (lb + 1) * LANES)
                piece = ct_ref[104 * part : 104 * part + LANES, lanes]
                c_ref[part, lanes, :] = piece.T


def finish_kernel(pieces_ref, momentum_ref, out_ref):
    width = momentum_ref.shape[1] // pieces_ref.shape[0]
    row = jnp.concatenate([pieces_ref[k][:, :width] for k in range(pieces_ref.shape[0])], axis=1)
    out_ref[...] = DECAY * momentum_ref[...] + row


def local(activations, grad_out, momentum):
    core = lax.axis_index("core")
    columns = grad_out.shape[1]
    share = columns // NR
    depth = activations.shape[1] // 2

    halves = activations.reshape(8, 2, depth).transpose(1, 0, 2)
    halves = jnp.broadcast_to(halves[None], (NR, 2, 8, depth)).reshape(2 * NR, 8, depth)
    halves = lax.all_to_all(halves, ("x", "z", "core"), 0, 0, tiled=True)
    acts = lax.all_gather(halves.reshape(NR * 16, depth), "y", axis=0, tiled=True)
    acts = acts.reshape(8, NR, 16, depth)

    own = lax.all_to_all(grad_out.T.reshape(NR, share, TOK), XZ, 0, 0, tiled=True)
    other = lax.ppermute(own, "core", CORES)

    grads, gram = pl.pallas_call(
        gram_kernel,
        grid=(NR,),
        in_specs=[
            pl.BlockSpec((1, share, TOK), lambda r: (r, 0, 0)),
            pl.BlockSpec((1, share, TOK), lambda r: (r, 0, 0)),
            pl.BlockSpec((8, 1, 16, depth), lambda r: (0, r, 0, 0)),
        ],
        out_specs=[
            pl.BlockSpec((1, 2 * share, depth), lambda r: (r, 0, 0)),
            pl.BlockSpec((8, LANES), lambda r: (0, 0)),
        ],
        out_shape=[
            jax.ShapeDtypeStruct((NR, 2 * share, depth), jnp.float32),
            jax.ShapeDtypeStruct((8, LANES), jnp.float32),
        ],
        scratch_shapes=[
            pltpu.VMEM((NR, 2 * share, depth), jnp.float32),
            pltpu.VMEM((1024, LANES), jnp.float32),
        ],
        name="gram",
    )(own, other, acts)

    gram = lax.all_to_all(jnp.broadcast_to(gram, (16, 8, LANES)), ("z", "core"), 0, 0, tiled=True)
    gram = jnp.sum(gram, axis=0)
    gram = lax.all_to_all(jnp.broadcast_to(gram, (32, 8, LANES)), ("x", "y"), 0, 0, tiled=True)

    block = 16
    combined = pl.pallas_call(
        combine_kernel,
        grid=(2 * share // block,),
        in_specs=[
            pl.BlockSpec((32, 8, LANES), lambda f: (0, 0, 0)),
            pl.BlockSpec((NR, block, depth), lambda f: (0, f, 0)),
        ],
        out_specs=pl.BlockSpec((2, depth, LANES), lambda f: (0, 0, 0)),
        out_shape=jax.ShapeDtypeStruct((2, depth, LANES), jnp.float32),
        scratch_shapes=[
            pltpu.VMEM((NR, LANES), jnp.float32),
            pltpu.VMEM((256, depth), jnp.float32),
        ],
        name="combine",
    )(gram, grads)

    mine = combined[0]
    came = lax.ppermute(combined[1], "core", CORES)
    low = jnp.where(core == 0, mine, came)
    high = jnp.where(core == 0, came, mine)
    pieces = jnp.concatenate([low, high], axis=0).reshape(NR, 24, LANES)
    pieces = lax.all_to_all(pieces, XZ, 0, 0, tiled=True)

    return pl.pallas_call(
        finish_kernel,
        out_shape=jax.ShapeDtypeStruct(momentum.shape, jnp.float32),
        name="finish",
    )(pieces, momentum)


def solution(mesh):
    devices = mesh.devices.reshape(4, 8, 8, 2)
    fine = Mesh(devices, ("x", "z", "y", "core"))
    dp, hidden = ("x", "z"), ("y", "core")
    return jax.shard_map(
        local,
        mesh=fine,
        in_specs=(P(dp + hidden, None), P(dp, hidden), P(dp, hidden)),
        out_specs=P(dp, hidden),
        check_vma=False,
    )
```

```python
import functools

import jax
import jax.numpy as jnp
from jax import lax
from jax.experimental import pallas as pl
from jax.experimental.pallas import tpu as pltpu
from jax.sharding import Mesh, PartitionSpec as P

EPSILON = 1e-06
DECAY = 0.9
NR = 32
TOK = 128
LANES = 128
XZ = ("x", "z")
CORES = [(0, 1), (1, 0)]
CHUNKS = ((0, 384),)


def gram_kernel(cols_ref, *refs):
    act_refs, (g_out_ref, gram_ref, g_ref, q_ref, sem) = refs[:-5], refs[-5:]
    groups = cols_ref.shape[1] // 8
    depth = act_refs[0].shape[-1]
    lane_blocks = depth // LANES
    unroll = 26 // lane_blocks

    def one(r, carry):
        act = jnp.concatenate([ref[r] for ref in act_refs], axis=0)
        g_ref[r] = jnp.dot(cols_ref[r], act, preferred_element_type=jnp.float32)
        return carry

    lax.fori_loop(0, NR, one, 0, unroll=16)
    save = pltpu.make_async_copy(g_ref, g_out_ref, sem)
    save.start()
    q_ref[...] = jnp.zeros_like(q_ref)

    def pair_block(rb, sb):
        def body(f, acc):
            acc = list(acc)
            for h in range(unroll):
                row = pl.multiple_of((f * unroll + h) * 8, 8)
                for lb in range(lane_blocks):
                    lanes = slice(lb * LANES, (lb + 1) * LANES)
                    left = [g_ref[rb * 4 + i, pl.ds(row, 8), lanes] for i in range(4)]
                    right = [g_ref[sb * 4 + i, pl.ds(row, 8), lanes] for i in range(4)]
                    for i in range(4):
                        for j in range(4):
                            acc[i * 4 + j] = acc[i * 4 + j] + left[i] * right[j]
            return tuple(acc)

        zero = jnp.zeros((8, LANES), jnp.float32)
        acc = lax.fori_loop(0, groups // unroll, body, (zero,) * 16)
        for i in range(4):
            left_id = rb * 4 + i
            base = lax.rem(left_id, 8) * 128 + lax.div(left_id, 8) * 32
            for j in range(4):
                q_ref[pl.ds(base + sb * 4 + j, 1), :] = jnp.sum(
                    acc[i * 4 + j], axis=0, keepdims=True
                )

    def outer(rb, carry):
        def inner(sb, c):
            pair_block(rb, sb)
            return c

        return lax.fori_loop(rb, NR // 4, inner, carry)

    lax.fori_loop(0, NR // 4, outer, 0)
    sums = lax.dot_general(
        jnp.ones((8, LANES), jnp.float32),
        q_ref[...],
        (((1,), (1,)), ((), ())),
        precision=lax.Precision.HIGHEST,
        preferred_element_type=jnp.float32,
    )
    for i in range(8):
        gram_ref[i : i + 1, :] = sums[i : i + 1, i * LANES : (i + 1) * LANES]
    save.wait()


def tree_weights(packed):
    gram = jnp.concatenate([packed[:, 32 * q : 32 * q + 32] for q in range(4)], axis=0)
    rows = lax.broadcasted_iota(jnp.int32, (NR, NR), 0)
    cols = lax.broadcasted_iota(jnp.int32, (NR, NR), 1)
    upper = jnp.where(rows < cols, gram, 0.0)
    quad = jnp.where(rows == cols, gram, 2.0 * upper)
    w_col = jnp.ones((NR, 1), jnp.float32)
    w_row = jnp.ones((1, NR), jnp.float32)
    for level in range(5):
        scale = w_col * w_row
        same_half = (rows >> level) == (cols >> level)
        same_pair = (rows >> (level + 1)) == (cols >> (level + 1))
        squares = jnp.where(same_half, quad * scale, 0.0)
        crosses = jnp.where(same_pair & (~same_half), upper * scale, 0.0)

        def both(values, mask):
            down = jnp.sum(values, axis=1, keepdims=True)
            across = jnp.sum(values, axis=0, keepdims=True)
            as_row = jnp.sum(jnp.where(mask, down, 0.0), axis=0, keepdims=True)
            as_col = jnp.sum(jnp.where(mask, across, 0.0), axis=1, keepdims=True)
            return as_col, as_row

        sq_col, sq_row = both(squares, same_half)
        cr_col, cr_row = both(crosses, same_pair)
        w_col = w_col * (1.0 - cr_col / (2.0 * (sq_col + EPSILON)))
        w_row = w_row * (1.0 - cr_row / (2.0 * (sq_row + EPSILON)))
    return w_col


def combine_kernel(part_ref, *refs):
    n = len(CHUNKS)
    kept, (mine_ref, theirs_ref, w_ref, ct_ref) = refs[:n], refs[n : n + 4]
    g_refs, sem = refs[n + 4 : -1], refs[-1]
    share = g_refs[0].shape[1] // 2
    loads = [pltpu.make_async_copy(kept[k], g_refs[k], sem.at[k]) for k in range(n)]
    for load in loads:
        load.start()
    weights = tree_weights(jnp.sum(part_ref[...], axis=0))
    for r in range(NR):
        w_ref[r] = jnp.broadcast_to(weights[r : r + 1, :], (8, LANES))
    ct_ref[pl.ds(2 * share, 48), :] = jnp.zeros((48, ct_ref.shape[1]), jnp.float32)
    for load in loads:
        load.wait()
    blocks = [(g, lb) for g in g_refs for lb in range(g.shape[2] // LANES)]

    def body(f, carry):
        row = pl.multiple_of(f * 8, 8)
        acc = [None] * len(blocks)
        for r in range(NR):
            weight = w_ref[r]
            for k, (g, lb) in enumerate(blocks):
                term = g[r, pl.ds(row, 8), lb * LANES : (lb + 1) * LANES] * weight
                acc[k] = term if r == 0 else acc[k] + term
        for k in range(len(blocks)):
            ct_ref[pl.ds(row, 8), k * LANES : (k + 1) * LANES] = acc[k]
        return carry

    lax.fori_loop(0, 2 * share // 8, body, 0)
    for part, ref in enumerate((mine_ref, theirs_ref)):
        for k in range(len(blocks)):
            lanes = slice(k * LANES, (k + 1) * LANES)
            ref[lanes, :] = ct_ref[share * part : share * part + LANES, lanes].T


def finish_kernel(pieces_ref, momentum_ref, out_ref):
    width = momentum_ref.shape[1] // pieces_ref.shape[0]
    row = jnp.concatenate([pieces_ref[k][:, :width] for k in range(pieces_ref.shape[0])], axis=1)
    out_ref[...] = DECAY * momentum_ref[...] + row


def ring(block):
    size = lax.axis_size("y")
    up = [(i, (i + 1) % size) for i in range(size)]
    down = [(i, (i - 1) % size) for i in range(size)]
    above, below = [block], [block]
    for step in range(size // 2):
        below.append(lax.ppermute(below[-1], "y", up))
        if step < size // 2 - 1:
            above.append(lax.ppermute(above[-1], "y", down))
    return above + below[:0:-1]


def local(activations, grad_out, momentum):
    core = lax.axis_index("core")
    columns = grad_out.shape[1]
    share = columns // NR
    depth = activations.shape[1] // 2

    halves = activations.reshape(8, 2, depth).transpose(1, 0, 2)
    halves = jnp.broadcast_to(halves[None], (NR, 2, 8, depth)).reshape(2 * NR, 8, depth)
    halves = lax.all_to_all(halves, ("x", "z", "core"), 0, 0, tiled=True)
    halves = halves.reshape(NR * 16, depth)

    shift = 16 * lax.axis_index("y")
    rolled = lax.dynamic_slice_in_dim(jnp.concatenate([grad_out, grad_out], axis=0), shift, TOK, 0)
    own = lax.all_to_all(rolled.T.reshape(NR, share, TOK), XZ, 0, 0, tiled=True)
    other = lax.ppermute(own, "core", CORES)
    cols = jnp.concatenate([own, other], axis=1)

    grads, grams = [], []
    for start, width in CHUNKS:
        acts = ring(halves[:, start : start + width].reshape(NR, 16, width))
        grad, gram = pl.pallas_call(
            gram_kernel,
            out_shape=[
                jax.ShapeDtypeStruct((NR, 2 * share, width), jnp.float32),
                jax.ShapeDtypeStruct((8, LANES), jnp.float32),
            ],
            out_specs=[
                pl.BlockSpec(memory_space=pltpu.HBM),
                pl.BlockSpec(memory_space=pltpu.VMEM),
            ],
            scratch_shapes=[
                pltpu.VMEM((NR, 2 * share, width), jnp.float32),
                pltpu.VMEM((1024, LANES), jnp.float32),
                pltpu.SemaphoreType.DMA,
            ],
            compiler_params=pltpu.CompilerParams(vmem_limit_bytes=60 << 20),
            name="gram",
        )(cols, *acts)
        grads.append(grad)
        grams.append(gram)
    gram = sum(grams)

    gram = lax.all_to_all(jnp.broadcast_to(gram, (16, 8, LANES)), ("z", "core"), 0, 0, tiled=True)
    gram = jnp.sum(gram, axis=0)
    gram = lax.all_to_all(jnp.broadcast_to(gram, (32, 8, LANES)), ("x", "y"), 0, 0, tiled=True)

    mine, theirs = pl.pallas_call(
        combine_kernel,
        out_shape=[jax.ShapeDtypeStruct((depth, LANES), jnp.float32)] * 2,
        scratch_shapes=[
            pltpu.VMEM((NR, 8, LANES), jnp.float32),
            pltpu.VMEM((256, depth), jnp.float32),
            *(pltpu.VMEM(g.shape, jnp.float32) for g in grads),
            pltpu.SemaphoreType.DMA((len(grads),)),
        ],
        in_specs=[pl.BlockSpec(memory_space=pltpu.VMEM)]
        + [pl.BlockSpec(memory_space=pltpu.HBM)] * len(grads),
        compiler_params=pltpu.CompilerParams(vmem_limit_bytes=60 << 20),
        name="combine",
    )(gram, *grads)
    came = lax.ppermute(theirs, "core", CORES)
    low = jnp.where(core == 0, mine, came)
    high = jnp.where(core == 0, came, mine)
    pieces = jnp.concatenate([low, high], axis=0).reshape(NR, 24, LANES)
    pieces = lax.all_to_all(pieces, XZ, 0, 0, tiled=True)

    return pl.pallas_call(
        finish_kernel,
        out_shape=jax.ShapeDtypeStruct(momentum.shape, jnp.float32),
        compiler_params=pltpu.CompilerParams(vmem_limit_bytes=4 << 20),
        name="finish",
    )(pieces, momentum)


def solution(mesh):
    devices = mesh.devices.reshape(4, 8, 8, 2)
    fine = Mesh(devices, ("x", "z", "y", "core"))
    dp, hidden = ("x", "z"), ("y", "core")
    return jax.shard_map(
        local,
        mesh=fine,
        in_specs=(P(dp + hidden, None), P(dp, hidden), P(dp, hidden)),
        out_specs=P(dp, hidden),
        check_vma=False,
    )
```

```python
import functools

import jax
import jax.numpy as jnp
from jax import lax
from jax.experimental import pallas as pl
from jax.experimental.pallas import tpu as pltpu
from jax.sharding import Mesh, PartitionSpec as P

EPSILON = 1e-06
DECAY = 0.9
NR = 32
TOK = 128
LANES = 128
XZ = ("x", "z")
CORES = [(0, 1), (1, 0)]
CHUNKS = ((0, 256), (256, 128))


def gram_kernel(cols_ref, *refs):
    act_refs, (g_out_ref, gram_ref, g_ref, q_ref, sem) = refs[:-5], refs[-5:]
    groups = cols_ref.shape[1] // 8
    depth = act_refs[0].shape[-1]
    lane_blocks = depth // LANES
    unroll = 26 if lane_blocks == 1 else 13
    assert groups % unroll == 0

    def one(r, carry):
        act = jnp.concatenate([ref[r] for ref in act_refs], axis=0)
        g_ref[r] = jnp.dot(cols_ref[r], act, preferred_element_type=jnp.float32)
        return carry

    lax.fori_loop(0, NR, one, 0, unroll=16)
    save = pltpu.make_async_copy(g_ref, g_out_ref, sem)
    save.start()
    q_ref[...] = jnp.zeros_like(q_ref)

    def pair_block(rb, sb):
        def body(f, acc):
            acc = list(acc)
            for h in range(unroll):
                row = pl.multiple_of((f * unroll + h) * 8, 8)
                for lb in range(lane_blocks):
                    lanes = slice(lb * LANES, (lb + 1) * LANES)
                    left = [g_ref[rb * 4 + i, pl.ds(row, 8), lanes] for i in range(4)]
                    right = [g_ref[sb * 4 + i, pl.ds(row, 8), lanes] for i in range(4)]
                    for i in range(4):
                        for j in range(4):
                            acc[i * 4 + j] = acc[i * 4 + j] + left[i] * right[j]
            return tuple(acc)

        zero = jnp.zeros((8, LANES), jnp.float32)
        acc = lax.fori_loop(0, groups // unroll, body, (zero,) * 16)
        for i in range(4):
            left_id = rb * 4 + i
            base = lax.rem(left_id, 8) * 128 + lax.div(left_id, 8) * 32
            for j in range(4):
                q_ref[pl.ds(base + sb * 4 + j, 1), :] = jnp.sum(
                    acc[i * 4 + j], axis=0, keepdims=True
                )

    def outer(rb, carry):
        def inner(sb, c):
            pair_block(rb, sb)
            return c

        return lax.fori_loop(rb, NR // 4, inner, carry)

    lax.fori_loop(0, NR // 4, outer, 0)
    sums = lax.dot_general(
        jnp.ones((8, LANES), jnp.float32),
        q_ref[...],
        (((1,), (1,)), ((), ())),
        precision=lax.Precision.HIGHEST,
        preferred_element_type=jnp.float32,
    )
    for i in range(8):
        gram_ref[i : i + 1, :] = sums[i : i + 1, i * LANES : (i + 1) * LANES]
    save.wait()


def tree_weights(packed):
    gram = jnp.concatenate([packed[:, 32 * q : 32 * q + 32] for q in range(4)], axis=0)
    rows = lax.broadcasted_iota(jnp.int32, (NR, NR), 0)
    cols = lax.broadcasted_iota(jnp.int32, (NR, NR), 1)
    upper = jnp.where(rows < cols, gram, 0.0)
    quad = jnp.where(rows == cols, gram, 2.0 * upper)
    w_col = jnp.ones((NR, 1), jnp.float32)
    w_row = jnp.ones((1, NR), jnp.float32)
    for level in range(5):
        scale = w_col * w_row
        same_half = (rows >> level) == (cols >> level)
        same_pair = (rows >> (level + 1)) == (cols >> (level + 1))
        squares = jnp.where(same_half, quad * scale, 0.0)
        crosses = jnp.where(same_pair & (~same_half), upper * scale, 0.0)

        def both(values, mask):
            down = jnp.sum(values, axis=1, keepdims=True)
            across = jnp.sum(values, axis=0, keepdims=True)
            as_row = jnp.sum(jnp.where(mask, down, 0.0), axis=0, keepdims=True)
            as_col = jnp.sum(jnp.where(mask, across, 0.0), axis=1, keepdims=True)
            return as_col, as_row

        sq_col, sq_row = both(squares, same_half)
        cr_col, cr_row = both(crosses, same_pair)
        w_col = w_col * (1.0 - cr_col / (2.0 * (sq_col + EPSILON)))
        w_row = w_row * (1.0 - cr_row / (2.0 * (sq_row + EPSILON)))
    return w_col


def combine_kernel(part_ref, *refs):
    n = len(CHUNKS)
    kept, (mine_ref, theirs_ref, w_ref, ct_ref) = refs[:n], refs[n : n + 4]
    g_refs, sem = refs[n + 4 : -1], refs[-1]
    share = g_refs[0].shape[1] // 2
    loads = [pltpu.make_async_copy(kept[k], g_refs[k], sem.at[k]) for k in range(n)]
    for load in loads:
        load.start()
    weights = tree_weights(jnp.sum(part_ref[...], axis=0))
    for r in range(NR):
        w_ref[r] = jnp.broadcast_to(weights[r : r + 1, :], (8, LANES))
    ct_ref[pl.ds(2 * share, 48), :] = jnp.zeros((48, ct_ref.shape[1]), jnp.float32)
    for load in loads:
        load.wait()
    blocks = [(g, lb) for g in g_refs for lb in range(g.shape[2] // LANES)]

    def body(f, carry):
        row = pl.multiple_of(f * 8, 8)
        acc = [None] * len(blocks)
        for r in range(NR):
            weight = w_ref[r]
            for k, (g, lb) in enumerate(blocks):
                term = g[r, pl.ds(row, 8), lb * LANES : (lb + 1) * LANES] * weight
                acc[k] = term if r == 0 else acc[k] + term
        for k in range(len(blocks)):
            ct_ref[pl.ds(row, 8), k * LANES : (k + 1) * LANES] = acc[k]
        return carry

    lax.fori_loop(0, 2 * share // 8, body, 0)
    for part, ref in enumerate((mine_ref, theirs_ref)):
        for k in range(len(blocks)):
            lanes = slice(k * LANES, (k + 1) * LANES)
            ref[lanes, :] = ct_ref[share * part : share * part + LANES, lanes].T


def finish_kernel(pieces_ref, momentum_ref, out_ref):
    width = momentum_ref.shape[1] // pieces_ref.shape[0]
    row = jnp.concatenate([pieces_ref[k][:, :width] for k in range(pieces_ref.shape[0])], axis=1)
    out_ref[...] = DECAY * momentum_ref[...] + row


def ring(block):
    size = lax.axis_size("y")
    up = [(i, (i + 1) % size) for i in range(size)]
    down = [(i, (i - 1) % size) for i in range(size)]
    above, below = [block], [block]
    for step in range(size // 2):
        below.append(lax.ppermute(below[-1], "y", up))
        if step < size // 2 - 1:
            above.append(lax.ppermute(above[-1], "y", down))
    return above + below[:0:-1]


def local(activations, grad_out, momentum):
    core = lax.axis_index("core")
    columns = grad_out.shape[1]
    share = columns // NR
    depth = activations.shape[1] // 2

    halves = activations.reshape(8, 2, depth).transpose(1, 0, 2)
    halves = jnp.broadcast_to(halves[None], (NR, 2, 8, depth)).reshape(2 * NR, 8, depth)
    halves = lax.all_to_all(halves, ("x", "z", "core"), 0, 0, tiled=True)
    halves = halves.reshape(NR * 16, depth)

    shift = 16 * lax.axis_index("y")
    rolled = lax.dynamic_slice_in_dim(jnp.concatenate([grad_out, grad_out], axis=0), shift, TOK, 0)
    own = lax.all_to_all(rolled.T.reshape(NR, share, TOK), XZ, 0, 0, tiled=True)
    other = lax.ppermute(own, "core", CORES)
    cols = jnp.concatenate([own, other], axis=1)

    grads, grams = [], []
    for start, width in CHUNKS:
        acts = ring(halves[:, start : start + width].reshape(NR, 16, width))
        grad, gram = pl.pallas_call(
            gram_kernel,
            out_shape=[
                jax.ShapeDtypeStruct((NR, 2 * share, width), jnp.float32),
                jax.ShapeDtypeStruct((8, LANES), jnp.float32),
            ],
            out_specs=[
                pl.BlockSpec(memory_space=pltpu.HBM),
                pl.BlockSpec(memory_space=pltpu.VMEM),
            ],
            scratch_shapes=[
                pltpu.VMEM((NR, 2 * share, width), jnp.float32),
                pltpu.VMEM((1024, LANES), jnp.float32),
                pltpu.SemaphoreType.DMA,
            ],
            compiler_params=pltpu.CompilerParams(vmem_limit_bytes=60 << 20),
            name="gram",
        )(cols, *acts)
        grads.append(grad)
        grams.append(gram)
    gram = sum(grams)

    gram = lax.all_to_all(jnp.broadcast_to(gram, (16, 8, LANES)), ("z", "core"), 0, 0, tiled=True)
    gram = jnp.sum(gram, axis=0)
    gram = lax.all_to_all(jnp.broadcast_to(gram, (32, 8, LANES)), ("x", "y"), 0, 0, tiled=True)

    mine, theirs = pl.pallas_call(
        combine_kernel,
        out_shape=[jax.ShapeDtypeStruct((depth, LANES), jnp.float32)] * 2,
        scratch_shapes=[
            pltpu.VMEM((NR, 8, LANES), jnp.float32),
            pltpu.VMEM((256, depth), jnp.float32),
            *(pltpu.VMEM(g.shape, jnp.float32) for g in grads),
            pltpu.SemaphoreType.DMA((len(grads),)),
        ],
        in_specs=[pl.BlockSpec(memory_space=pltpu.VMEM)]
        + [pl.BlockSpec(memory_space=pltpu.HBM)] * len(grads),
        compiler_params=pltpu.CompilerParams(vmem_limit_bytes=60 << 20),
        name="combine",
    )(gram, *grads)
    came = lax.ppermute(theirs, "core", CORES)
    low = jnp.where(core == 0, mine, came)
    high = jnp.where(core == 0, came, mine)
    pieces = jnp.concatenate([low, high], axis=0).reshape(NR, 24, LANES)
    pieces = lax.all_to_all(pieces, XZ, 0, 0, tiled=True)

    return pl.pallas_call(
        finish_kernel,
        out_shape=jax.ShapeDtypeStruct(momentum.shape, jnp.float32),
        compiler_params=pltpu.CompilerParams(vmem_limit_bytes=4 << 20),
        name="finish",
    )(pieces, momentum)


def solution(mesh):
    devices = mesh.devices.reshape(4, 8, 8, 2)
    fine = Mesh(devices, ("x", "z", "y", "core"))
    dp, hidden = ("x", "z"), ("y", "core")
    return jax.shard_map(
        local,
        mesh=fine,
        in_specs=(P(dp + hidden, None), P(dp, hidden), P(dp, hidden)),
        out_specs=P(dp, hidden),
        check_vma=False,
    )
```

```python
import jax
import jax.numpy as jnp
from jax import lax
from jax.experimental import pallas as pl
from jax.experimental.pallas import tpu as pltpu
from jax.sharding import Mesh, PartitionSpec as P


EPSILON = 1e-06
DECAY = 0.9
NR = 32
TOK = 128
LANES = 128
XZ = ("x", "z")
CORES = [(0, 1), (1, 0)]
PIECES = ((0, 56), (56, 56), (112, 56), (168, 40))


def gram_kernel(cols_ref, *refs):
    act_refs, (g_out_ref, gram_ref, g_ref, q_ref, sem) = refs[:-5], refs[-5:]
    groups = cols_ref.shape[1] // 8
    depth = act_refs[0].shape[-1]
    lane_blocks = depth // LANES
    unroll = 26 if lane_blocks == 1 else 13
    assert groups % unroll == 0

    def one(r, carry):
        act = jnp.concatenate([ref[r] for ref in act_refs], axis=0)
        g_ref[r] = jnp.dot(cols_ref[r], act, preferred_element_type=jnp.float32)
        return carry

    lax.fori_loop(0, NR, one, 0, unroll=16)
    save = pltpu.make_async_copy(g_ref, g_out_ref, sem)
    save.start()
    q_ref[...] = jnp.zeros_like(q_ref)

    def pair_block(rb, sb):
        def body(f, acc):
            acc = list(acc)
            for h in range(unroll):
                row = pl.multiple_of((f * unroll + h) * 8, 8)
                for lb in range(lane_blocks):
                    lanes = slice(lb * LANES, (lb + 1) * LANES)
                    left = [g_ref[rb * 4 + i, pl.ds(row, 8), lanes] for i in range(4)]
                    right = [g_ref[sb * 4 + i, pl.ds(row, 8), lanes] for i in range(4)]
                    for i in range(4):
                        for j in range(4):
                            acc[i * 4 + j] = acc[i * 4 + j] + left[i] * right[j]
            return tuple(acc)

        zero = jnp.zeros((8, LANES), jnp.float32)
        acc = lax.fori_loop(0, groups // unroll, body, (zero,) * 16)
        for i in range(4):
            left_id = rb * 4 + i
            base = lax.rem(left_id, 8) * 128 + lax.div(left_id, 8) * 32
            for j in range(4):
                q_ref[pl.ds(base + sb * 4 + j, 1), :] = jnp.sum(
                    acc[i * 4 + j], axis=0, keepdims=True
                )

    def outer(rb, carry):
        def inner(sb, c):
            pair_block(rb, sb)
            return c

        return lax.fori_loop(rb, NR // 4, inner, carry)

    lax.fori_loop(0, NR // 4, outer, 0)
    sums = lax.dot_general(
        jnp.ones((8, LANES), jnp.float32),
        q_ref[...],
        (((1,), (1,)), ((), ())),
        precision=lax.Precision.HIGHEST,
        preferred_element_type=jnp.float32,
    )
    for i in range(8):
        gram_ref[i : i + 1, :] = sums[i : i + 1, i * LANES : (i + 1) * LANES]
    save.wait()


def tree_weights(packed):
    gram = jnp.concatenate([packed[:, 32 * q : 32 * q + 32] for q in range(4)], axis=0)
    rows = lax.broadcasted_iota(jnp.int32, (NR, NR), 0)
    cols = lax.broadcasted_iota(jnp.int32, (NR, NR), 1)
    upper = jnp.where(rows < cols, gram, 0.0)
    quad = jnp.where(rows == cols, gram, 2.0 * upper)
    w_col = jnp.ones((NR, 1), jnp.float32)
    w_row = jnp.ones((1, NR), jnp.float32)
    for level in range(5):
        scale = w_col * w_row
        same_half = (rows >> level) == (cols >> level)
        same_pair = (rows >> (level + 1)) == (cols >> (level + 1))
        squares = jnp.where(same_half, quad * scale, 0.0)
        crosses = jnp.where(same_pair & (~same_half), upper * scale, 0.0)

        def both(values, mask):
            down = jnp.sum(values, axis=1, keepdims=True)
            across = jnp.sum(values, axis=0, keepdims=True)
            as_row = jnp.sum(jnp.where(mask, down, 0.0), axis=0, keepdims=True)
            as_col = jnp.sum(jnp.where(mask, across, 0.0), axis=1, keepdims=True)
            return as_col, as_row

        sq_col, sq_row = both(squares, same_half)
        cr_col, cr_row = both(crosses, same_pair)
        w_col = w_col * (1.0 - cr_col / (2.0 * (sq_col + EPSILON)))
        w_row = w_row * (1.0 - cr_row / (2.0 * (sq_row + EPSILON)))
    return w_col


def combine_kernel(part_ref, kept_ref, mine_ref, theirs_ref, w_ref, ct_ref, g_ref, sem):
    share = kept_ref.shape[1] // 2
    lane_blocks = kept_ref.shape[2] // LANES
    loads = []
    for k, (start, size) in enumerate(PIECES):
        rows = pl.ds(start, size)
        loads.append(pltpu.make_async_copy(kept_ref.at[:, rows], g_ref.at[:, rows], sem.at[k]))
        loads[-1].start()
    weights = tree_weights(jnp.sum(part_ref[...], axis=0))
    for r in range(NR):
        w_ref[r] = jnp.broadcast_to(weights[r : r + 1, :], (8, LANES))
    ct_ref[pl.ds(2 * share, 48), :] = jnp.zeros((48, ct_ref.shape[1]), jnp.float32)

    def body(f, carry):
        row = pl.multiple_of(f * 8, 8)
        acc = [None] * lane_blocks
        for r in range(NR):
            weight = w_ref[r]
            for k in range(lane_blocks):
                term = g_ref[r, pl.ds(row, 8), k * LANES : (k + 1) * LANES] * weight
                acc[k] = term if r == 0 else acc[k] + term
        for k in range(lane_blocks):
            ct_ref[pl.ds(row, 8), k * LANES : (k + 1) * LANES] = acc[k]
        return carry

    for load, (start, size) in zip(loads, PIECES):
        load.wait()
        lax.fori_loop(start // 8, (start + size) // 8, body, 0)
    for part, ref in enumerate((mine_ref, theirs_ref)):
        for k in range(lane_blocks):
            lanes = slice(k * LANES, (k + 1) * LANES)
            ref[lanes, :] = ct_ref[share * part : share * part + LANES, lanes].T


def finish_kernel(pieces_ref, momentum_ref, out_ref):
    width = momentum_ref.shape[1] // pieces_ref.shape[0]
    row = jnp.concatenate([pieces_ref[k][:, :width] for k in range(pieces_ref.shape[0])], axis=1)
    out_ref[...] = DECAY * momentum_ref[...] + row


def ring(block):
    size = lax.axis_size("y")
    up = [(i, (i + 1) % size) for i in range(size)]
    down = [(i, (i - 1) % size) for i in range(size)]
    above, below = [block], [block]
    for step in range(size // 2):
        below.append(lax.ppermute(below[-1], "y", up))
        if step < size // 2 - 1:
            above.append(lax.ppermute(above[-1], "y", down))
    return above + below[:0:-1]


def local(activations, grad_out, momentum):
    core = lax.axis_index("core")
    columns = grad_out.shape[1]
    share = columns // NR
    depth = activations.shape[1] // 2

    halves = activations.reshape(8, 2, depth).transpose(1, 0, 2)
    halves = jnp.broadcast_to(halves[None], (NR, 2, 8, depth)).reshape(2 * NR, 8, depth)
    halves = lax.all_to_all(halves, ("x", "z", "core"), 0, 0, tiled=True)
    halves = halves.reshape(NR * 16, depth)

    shift = 16 * lax.axis_index("y")
    rolled = lax.dynamic_slice_in_dim(jnp.concatenate([grad_out, grad_out], axis=0), shift, TOK, 0)
    acts = ring(halves.reshape(NR, 16, depth))
    own = lax.all_to_all(rolled.T.reshape(NR, share, TOK), XZ, 0, 0, tiled=True)
    other = lax.ppermute(own, "core", CORES)
    cols = jnp.concatenate([own, other], axis=1)

    grads, gram = pl.pallas_call(
        gram_kernel,
        out_shape=[
            jax.ShapeDtypeStruct((NR, 2 * share, depth), jnp.float32),
            jax.ShapeDtypeStruct((8, LANES), jnp.float32),
        ],
        out_specs=[
            pl.BlockSpec(memory_space=pltpu.HBM),
            pl.BlockSpec(memory_space=pltpu.VMEM),
        ],
        scratch_shapes=[
            pltpu.VMEM((NR, 2 * share, depth), jnp.float32),
            pltpu.VMEM((1024, LANES), jnp.float32),
            pltpu.SemaphoreType.DMA,
        ],
        compiler_params=pltpu.CompilerParams(vmem_limit_bytes=60 << 20),
        name="gram",
    )(cols, *acts)

    gram = lax.all_to_all(jnp.broadcast_to(gram, (16, 8, LANES)), ("z", "core"), 0, 0, tiled=True)
    gram = jnp.sum(gram, axis=0)
    gram = lax.all_to_all(jnp.broadcast_to(gram, (32, 8, LANES)), ("x", "y"), 0, 0, tiled=True)

    mine, theirs = pl.pallas_call(
        combine_kernel,
        out_shape=[jax.ShapeDtypeStruct((depth, LANES), jnp.float32)] * 2,
        scratch_shapes=[
            pltpu.VMEM((NR, 8, LANES), jnp.float32),
            pltpu.VMEM((256, depth), jnp.float32),
            pltpu.VMEM(grads.shape, jnp.float32),
            pltpu.SemaphoreType.DMA((len(PIECES),)),
        ],
        in_specs=[
            pl.BlockSpec(memory_space=pltpu.VMEM),
            pl.BlockSpec(memory_space=pltpu.HBM),
        ],
        compiler_params=pltpu.CompilerParams(vmem_limit_bytes=60 << 20),
        name="combine",
    )(gram, grads)
    came = lax.ppermute(theirs, "core", CORES)
    low = jnp.where(core == 0, mine, came)
    high = jnp.where(core == 0, came, mine)
    pieces = jnp.concatenate([low, high], axis=0).reshape(NR, 24, LANES)
    pieces = lax.all_to_all(pieces, XZ, 0, 0, tiled=True)

    return pl.pallas_call(
        finish_kernel,
        out_shape=jax.ShapeDtypeStruct(momentum.shape, jnp.float32),
        compiler_params=pltpu.CompilerParams(vmem_limit_bytes=4 << 20),
        name="finish",
    )(pieces, momentum)


def solution(mesh):
    devices = mesh.devices.reshape(4, 8, 8, 2)
    fine = Mesh(devices, ("x", "z", "y", "core"))
    dp, hidden = ("x", "z"), ("y", "core")

    return jax.shard_map(
        local,
        mesh=fine,
        in_specs=(P(dp + hidden, None), P(dp, hidden), P(dp, hidden)),
        out_specs=P(dp, hidden),
        check_vma=False,
    )
```

```python
import jax
import jax.numpy as jnp
from jax import lax
from jax.experimental import pallas as pl
from jax.experimental.pallas import tpu as pltpu
from jax.sharding import Mesh, PartitionSpec as P


EPSILON = 1e-06
DECAY = 0.9
NR = 32
TOK = 128
LANES = 128
XZ = ("x", "z")
CORES = [(0, 1), (1, 0)]
PIECES = ((0, 56), (56, 56), (112, 56), (168, 40))


def gram_kernel(cols_ref, *refs):
    act_refs, (g_out_ref, gram_ref, g_ref, q_ref, sem) = refs[:-5], refs[-5:]
    groups = cols_ref.shape[1] // 8
    depth = act_refs[0].shape[-1]
    lane_blocks = depth // LANES
    unroll = 26
    assert groups % unroll == 0

    opposite = len(act_refs) // 2
    for r in range(NR):
        half = r // (NR // 2)
        parts = act_refs[:opposite] + act_refs[opposite + half : opposite + half + 1]
        rows = [ref[r % ref.shape[0]] for ref in parts + act_refs[opposite + 2 :]]
        act = jnp.concatenate(rows, axis=0)
        g_ref[r] = jnp.dot(cols_ref[r], act, preferred_element_type=jnp.float32)

    save = pltpu.make_async_copy(g_ref, g_out_ref, sem)
    save.start()
    q_ref[...] = jnp.zeros_like(q_ref)

    def pair_block(rb, sb, same):
        pairs = [(i, j) for i in range(4) for j in range(4) if not same or i <= j]

        def body(f, acc):
            acc = list(acc)
            for h in range(unroll):
                row = pl.multiple_of((f * unroll + h) * 8, 8)
                for lb in range(lane_blocks):
                    lanes = slice(lb * LANES, (lb + 1) * LANES)
                    left = [g_ref[rb * 4 + i, pl.ds(row, 8), lanes] for i in range(4)]
                    right = left
                    if not same:
                        right = [g_ref[sb * 4 + i, pl.ds(row, 8), lanes] for i in range(4)]
                    for n, (i, j) in enumerate(pairs):
                        acc[n] = acc[n] + left[i] * right[j]
            return tuple(acc)

        zero = jnp.zeros((8, LANES), jnp.float32)
        acc = lax.fori_loop(0, groups // unroll, body, (zero,) * len(pairs))
        for n, (i, j) in enumerate(pairs):
            left_id = rb * 4 + i
            base = lax.rem(left_id, 8) * 128 + lax.div(left_id, 8) * 32
            q_ref[pl.ds(base + sb * 4 + j, 1), :] = jnp.sum(acc[n], axis=0, keepdims=True)

    def outer(rb, carry):
        pair_block(rb, rb, True)

        def inner(sb, c):
            pair_block(rb, sb, False)
            return c

        return lax.fori_loop(rb + 1, NR // 4, inner, carry)

    lax.fori_loop(0, NR // 4, outer, 0)
    sums = lax.dot_general(
        jnp.ones((8, LANES), jnp.float32),
        q_ref[...],
        (((1,), (1,)), ((), ())),
        precision=lax.Precision.HIGHEST,
        preferred_element_type=jnp.float32,
    )
    for i in range(8):
        row = sums[i : i + 1, i * LANES : (i + 1) * LANES]
        for k in range(gram_ref.shape[0]):
            gram_ref[k, i : i + 1, :] = row
    save.wait()


def tree_weights(packed):
    gram = jnp.concatenate([packed[:, 32 * q : 32 * q + 32] for q in range(4)], axis=0)
    rows = lax.broadcasted_iota(jnp.int32, (NR, NR), 0)
    cols = lax.broadcasted_iota(jnp.int32, (NR, NR), 1)
    upper = jnp.where(rows < cols, gram, 0.0)
    quad = jnp.where(rows == cols, gram, 2.0 * upper)
    w_col = jnp.ones((NR, 1), jnp.float32)
    w_row = jnp.ones((1, NR), jnp.float32)
    for level in range(5):
        scale = w_col * w_row
        same_half = (rows >> level) == (cols >> level)
        same_pair = (rows >> (level + 1)) == (cols >> (level + 1))
        squares = jnp.where(same_half, quad * scale, 0.0)
        crosses = jnp.where(same_pair & (~same_half), upper * scale, 0.0)

        def both(values, mask):
            down = jnp.sum(values, axis=1, keepdims=True)
            across = jnp.sum(values, axis=0, keepdims=True)
            as_row = jnp.sum(jnp.where(mask, down, 0.0), axis=0, keepdims=True)
            as_col = jnp.sum(jnp.where(mask, across, 0.0), axis=1, keepdims=True)
            return as_col, as_row

        sq_col, sq_row = both(squares, same_half)
        cr_col, cr_row = both(crosses, same_pair)
        w_col = w_col * (1.0 - cr_col / (2.0 * (sq_col + EPSILON)))
        w_row = w_row * (1.0 - cr_row / (2.0 * (sq_row + EPSILON)))
    return w_col


def combine_kernel(part_ref, kept_ref, mine_ref, theirs_ref, w_ref, ct_ref, g_ref, sem):
    share = kept_ref.shape[1] // 2
    lane_blocks = kept_ref.shape[2] // LANES
    loads = []
    for k, (start, size) in enumerate(PIECES):
        rows = pl.ds(start, size)
        loads.append(pltpu.make_async_copy(kept_ref.at[:, rows], g_ref.at[:, rows], sem.at[k]))
        loads[-1].start()
    weights = tree_weights(jnp.sum(part_ref[...], axis=0))
    for r in range(NR):
        w_ref[r] = jnp.broadcast_to(weights[r : r + 1, :], (8, LANES))
    ct_ref[pl.ds(2 * share, 48), :] = jnp.zeros((48, ct_ref.shape[1]), jnp.float32)

    def body(f, carry):
        row = pl.multiple_of(f * 8, 8)
        acc = [None] * lane_blocks
        for r in range(NR):
            weight = w_ref[r]
            for k in range(lane_blocks):
                term = g_ref[r, pl.ds(row, 8), k * LANES : (k + 1) * LANES] * weight
                acc[k] = term if r == 0 else acc[k] + term
        for k in range(lane_blocks):
            ct_ref[pl.ds(row, 8), k * LANES : (k + 1) * LANES] = acc[k]
        return carry

    for load, (start, size) in zip(loads, PIECES):
        load.wait()
        lax.fori_loop(start // 8, (start + size) // 8, body, 0)
    for part, ref in enumerate((mine_ref, theirs_ref)):
        for k in range(lane_blocks):
            lanes = slice(k * LANES, (k + 1) * LANES)
            ref[lanes, :] = ct_ref[share * part : share * part + LANES, lanes].T


def finish_kernel(pieces_ref, momentum_ref, out_ref):
    width = momentum_ref.shape[1] // pieces_ref.shape[0]
    row = jnp.concatenate([pieces_ref[k][:, :width] for k in range(pieces_ref.shape[0])], axis=1)
    out_ref[...] = DECAY * momentum_ref[...] + row


def ring(block):
    size = lax.axis_size("y")
    half = block.shape[0] // 2
    up = [(i, (i + 1) % size) for i in range(size)]
    down = [(i, (i - 1) % size) for i in range(size)]
    above, below = [block], [block]
    for step in range(size // 2):
        last = step == size // 2 - 1
        from_below, from_above = below[-1], above[-1]
        if last:
            from_below, from_above = from_below[:half], from_above[half:]
        below.append(lax.ppermute(from_below, "y", up))
        above.append(lax.ppermute(from_above, "y", down))
    return above[:-1] + [below[-1], above[-1]] + below[-2:0:-1]


def local(activations, grad_out, momentum):
    core = lax.axis_index("core")
    columns = grad_out.shape[1]
    share = columns // NR
    depth = activations.shape[1] // 2

    halves = activations.reshape(8, 2, depth).transpose(1, 0, 2)
    halves = jnp.broadcast_to(halves[None], (NR, 2, 8, depth)).reshape(2 * NR, 8, depth)
    halves = lax.all_to_all(halves, ("x", "z", "core"), 0, 0, tiled=True)
    halves = halves.reshape(NR * 16, depth)

    shift = 16 * lax.axis_index("y")
    rolled = lax.dynamic_slice_in_dim(jnp.concatenate([grad_out, grad_out], axis=0), shift, TOK, 0)
    acts = ring(halves.reshape(NR, 16, depth))
    own = lax.all_to_all(rolled.T.reshape(NR, share, TOK), XZ, 0, 0, tiled=True)
    other = lax.ppermute(own, "core", CORES)
    cols = jnp.concatenate([own, other], axis=1)

    grads, gram = pl.pallas_call(
        gram_kernel,
        out_shape=[
            jax.ShapeDtypeStruct((NR, 2 * share, depth), jnp.float32),
            jax.ShapeDtypeStruct((16, 8, LANES), jnp.float32),
        ],
        out_specs=[
            pl.BlockSpec(memory_space=pltpu.HBM),
            pl.BlockSpec(memory_space=pltpu.VMEM),
        ],
        scratch_shapes=[
            pltpu.VMEM((NR, 2 * share, depth), jnp.float32),
            pltpu.VMEM((1024, LANES), jnp.float32),
            pltpu.SemaphoreType.DMA,
        ],
        compiler_params=pltpu.CompilerParams(vmem_limit_bytes=48 << 20),
        name="gram",
    )(cols, *acts)

    gram = lax.all_to_all(gram, ("z", "core"), 0, 0, tiled=True)
    gram = jnp.sum(gram, axis=0)
    gram = lax.all_to_all(jnp.broadcast_to(gram, (32, 8, LANES)), ("x", "y"), 0, 0, tiled=True)

    mine, theirs = pl.pallas_call(
        combine_kernel,
        out_shape=[jax.ShapeDtypeStruct((depth, LANES), jnp.float32)] * 2,
        scratch_shapes=[
            pltpu.VMEM((NR, 8, LANES), jnp.float32),
            pltpu.VMEM((256, depth), jnp.float32),
            pltpu.VMEM(grads.shape, jnp.float32),
            pltpu.SemaphoreType.DMA((len(PIECES),)),
        ],
        in_specs=[
            pl.BlockSpec(memory_space=pltpu.VMEM),
            pl.BlockSpec(memory_space=pltpu.HBM),
        ],
        compiler_params=pltpu.CompilerParams(vmem_limit_bytes=56 << 20),
        name="combine",
    )(gram, grads)
    came = lax.ppermute(theirs, "core", CORES)
    low = jnp.where(core == 0, mine, came)
    high = jnp.where(core == 0, came, mine)
    pieces = jnp.concatenate([low, high], axis=0).reshape(NR, 24, LANES)
    pieces = lax.all_to_all(pieces, XZ, 0, 0, tiled=True)

    return pl.pallas_call(
        finish_kernel,
        out_shape=jax.ShapeDtypeStruct(momentum.shape, jnp.float32),
        compiler_params=pltpu.CompilerParams(vmem_limit_bytes=4 << 20),
        name="finish",
    )(pieces, momentum)


def solution(mesh):
    devices = mesh.devices.reshape(4, 8, 8, 2)
    fine = Mesh(devices, ("x", "z", "y", "core"))
    dp, hidden = ("x", "z"), ("y", "core")

    return jax.shard_map(
        local,
        mesh=fine,
        in_specs=(P(dp + hidden, None), P(dp, hidden), P(dp, hidden)),
        out_specs=P(dp, hidden),
        check_vma=False,
    )
```

```python
import jax
import jax.numpy as jnp
from jax import lax
from jax.experimental import pallas as pl
from jax.experimental.pallas import tpu as pltpu
from jax.sharding import Mesh, PartitionSpec as P


EPSILON = 1e-06
DECAY = 0.9
NR = 32
TOK = 128
LANES = 128
XZ = ("x", "z")
CORES = [(0, 1), (1, 0)]
PIECES = ((0, 56), (56, 56), (112, 56), (168, 40))


def gram_kernel(cols_ref, *refs):
    act_refs, (g_out_ref, gram_ref, g_ref, q_ref, sem) = refs[:-5], refs[-5:]
    groups = cols_ref.shape[1] // 8
    depth = act_refs[0].shape[-1]
    lane_blocks = depth // LANES
    unroll = 26
    assert groups % unroll == 0

    def one(r, carry):
        act = jnp.concatenate([ref[r] for ref in act_refs], axis=0)
        g_ref[r] = jnp.dot(cols_ref[r], act, preferred_element_type=jnp.float32)
        return carry

    lax.fori_loop(0, NR, one, 0, unroll=NR)
    save = pltpu.make_async_copy(g_ref, g_out_ref, sem)
    save.start()
    q_ref[...] = jnp.zeros_like(q_ref)

    def pair_block(rb, sb, same):
        pairs = [(i, j) for i in range(4) for j in range(4) if not same or i <= j]

        def body(f, acc):
            acc = list(acc)
            for h in range(unroll):
                row = pl.multiple_of((f * unroll + h) * 8, 8)
                for lb in range(lane_blocks):
                    lanes = slice(lb * LANES, (lb + 1) * LANES)
                    left = [g_ref[rb * 4 + i, pl.ds(row, 8), lanes] for i in range(4)]
                    right = left
                    if not same:
                        right = [g_ref[sb * 4 + i, pl.ds(row, 8), lanes] for i in range(4)]
                    for n, (i, j) in enumerate(pairs):
                        acc[n] = acc[n] + left[i] * right[j]
            return tuple(acc)

        zero = jnp.zeros((8, LANES), jnp.float32)
        acc = lax.fori_loop(0, groups // unroll, body, (zero,) * len(pairs))
        for n, (i, j) in enumerate(pairs):
            left_id = rb * 4 + i
            base = lax.rem(left_id, 8) * 128 + lax.div(left_id, 8) * 32
            q_ref[pl.ds(base + sb * 4 + j, 1), :] = jnp.sum(acc[n], axis=0, keepdims=True)

    def outer(rb, carry):
        pair_block(rb, rb, True)

        def inner(sb, c):
            pair_block(rb, sb, False)
            return c

        return lax.fori_loop(rb + 1, NR // 4, inner, carry)

    lax.fori_loop(0, NR // 4, outer, 0)
    sums = lax.dot_general(
        jnp.ones((8, LANES), jnp.float32),
        q_ref[...],
        (((1,), (1,)), ((), ())),
        precision=lax.Precision.HIGHEST,
        preferred_element_type=jnp.float32,
    )
    for i in range(8):
        row = sums[i : i + 1, i * LANES : (i + 1) * LANES]
        for k in range(gram_ref.shape[0]):
            gram_ref[k, i : i + 1, :] = row
    save.wait()


def tree_weights(packed):
    gram = jnp.concatenate([packed[:, 32 * q : 32 * q + 32] for q in range(4)], axis=0)
    rows = lax.broadcasted_iota(jnp.int32, (NR, NR), 0)
    cols = lax.broadcasted_iota(jnp.int32, (NR, NR), 1)
    upper = jnp.where(rows < cols, gram, 0.0)
    quad = jnp.where(rows == cols, gram, 2.0 * upper)
    w_col = jnp.ones((NR, 1), jnp.float32)
    w_row = jnp.ones((1, NR), jnp.float32)
    for level in range(5):
        scale = w_col * w_row
        same_half = (rows >> level) == (cols >> level)
        same_pair = (rows >> (level + 1)) == (cols >> (level + 1))
        squares = jnp.where(same_half, quad * scale, 0.0)
        crosses = jnp.where(same_pair & (~same_half), upper * scale, 0.0)

        def both(values, mask):
            down = jnp.sum(values, axis=1, keepdims=True)
            across = jnp.sum(values, axis=0, keepdims=True)
            as_row = jnp.sum(jnp.where(mask, down, 0.0), axis=0, keepdims=True)
            as_col = jnp.sum(jnp.where(mask, across, 0.0), axis=1, keepdims=True)
            return as_col, as_row

        sq_col, sq_row = both(squares, same_half)
        cr_col, cr_row = both(crosses, same_pair)
        w_col = w_col * (1.0 - cr_col / (2.0 * (sq_col + EPSILON)))
        w_row = w_row * (1.0 - cr_row / (2.0 * (sq_row + EPSILON)))
    return w_col


def combine_kernel(part_ref, kept_ref, mine_ref, theirs_ref, w_ref, ct_ref, g_ref, sem):
    share = kept_ref.shape[1] // 2
    lane_blocks = kept_ref.shape[2] // LANES
    loads = []
    for k, (start, size) in enumerate(PIECES):
        rows = pl.ds(start, size)
        loads.append(pltpu.make_async_copy(kept_ref.at[:, rows], g_ref.at[:, rows], sem.at[k]))
        loads[-1].start()
    weights = tree_weights(jnp.sum(part_ref[...], axis=0))
    for r in range(NR):
        w_ref[r] = jnp.broadcast_to(weights[r : r + 1, :], (8, LANES))
    ct_ref[pl.ds(2 * share, 48), :] = jnp.zeros((48, ct_ref.shape[1]), jnp.float32)

    def body(f, carry):
        row = pl.multiple_of(f * 8, 8)
        acc = [None] * lane_blocks
        for r in range(NR):
            weight = w_ref[r]
            for k in range(lane_blocks):
                term = g_ref[r, pl.ds(row, 8), k * LANES : (k + 1) * LANES] * weight
                acc[k] = term if r == 0 else acc[k] + term
        for k in range(lane_blocks):
            ct_ref[pl.ds(row, 8), k * LANES : (k + 1) * LANES] = acc[k]
        return carry

    for load, (start, size) in zip(loads, PIECES):
        load.wait()
        lax.fori_loop(start // 8, (start + size) // 8, body, 0)
    for part, ref in enumerate((mine_ref, theirs_ref)):
        for k in range(lane_blocks):
            lanes = slice(k * LANES, (k + 1) * LANES)
            ref[lanes, :] = ct_ref[share * part : share * part + LANES, lanes].T


def finish_kernel(pieces_ref, momentum_ref, out_ref):
    width = momentum_ref.shape[1] // pieces_ref.shape[0]
    row = jnp.concatenate([pieces_ref[k][:, :width] for k in range(pieces_ref.shape[0])], axis=1)
    out_ref[...] = DECAY * momentum_ref[...] + row


def ring(block):
    size = lax.axis_size("y")
    up = [(i, (i + 1) % size) for i in range(size)]
    down = [(i, (i - 1) % size) for i in range(size)]
    above, below = [block], [block]
    for step in range(size // 2):
        below.append(lax.ppermute(below[-1], "y", up))
        if step < size // 2 - 1:
            above.append(lax.ppermute(above[-1], "y", down))
    return above + below[:0:-1]


def local(activations, grad_out, momentum):
    core = lax.axis_index("core")
    columns = grad_out.shape[1]
    share = columns // NR
    depth = activations.shape[1] // 2

    halves = activations.reshape(8, 2, depth).transpose(1, 0, 2)
    halves = jnp.broadcast_to(halves[None], (NR, 2, 8, depth)).reshape(2 * NR, 8, depth)
    halves = lax.all_to_all(halves, ("x", "z", "core"), 0, 0, tiled=True)
    halves = halves.reshape(NR * 16, depth)

    shift = 16 * lax.axis_index("y")
    rolled = lax.dynamic_slice_in_dim(jnp.concatenate([grad_out, grad_out], axis=0), shift, TOK, 0)
    acts = ring(halves.reshape(NR, 16, depth))
    own = lax.all_to_all(rolled.T.reshape(NR, share, TOK), XZ, 0, 0, tiled=True)
    other = lax.ppermute(own, "core", CORES)
    cols = jnp.concatenate([own, other], axis=1)

    grads, gram = pl.pallas_call(
        gram_kernel,
        out_shape=[
            jax.ShapeDtypeStruct((NR, 2 * share, depth), jnp.float32),
            jax.ShapeDtypeStruct((16, 8, LANES), jnp.float32),
        ],
        out_specs=[
            pl.BlockSpec(memory_space=pltpu.HBM),
            pl.BlockSpec(memory_space=pltpu.VMEM),
        ],
        scratch_shapes=[
            pltpu.VMEM((NR, 2 * share, depth), jnp.float32),
            pltpu.VMEM((1024, LANES), jnp.float32),
            pltpu.SemaphoreType.DMA,
        ],
        compiler_params=pltpu.CompilerParams(vmem_limit_bytes=48 << 20),
        name="gram",
    )(cols, *acts)

    gram = lax.all_to_all(gram, ("z", "core"), 0, 0, tiled=True)
    gram = jnp.sum(gram, axis=0)
    gram = lax.all_to_all(jnp.broadcast_to(gram, (32, 8, LANES)), ("x", "y"), 0, 0, tiled=True)

    mine, theirs = pl.pallas_call(
        combine_kernel,
        out_shape=[jax.ShapeDtypeStruct((depth, LANES), jnp.float32)] * 2,
        scratch_shapes=[
            pltpu.VMEM((NR, 8, LANES), jnp.float32),
            pltpu.VMEM((256, depth), jnp.float32),
            pltpu.VMEM(grads.shape, jnp.float32),
            pltpu.SemaphoreType.DMA((len(PIECES),)),
        ],
        in_specs=[
            pl.BlockSpec(memory_space=pltpu.VMEM),
            pl.BlockSpec(memory_space=pltpu.HBM),
        ],
        compiler_params=pltpu.CompilerParams(vmem_limit_bytes=48 << 20),
        name="combine",
    )(gram, grads)
    came = lax.ppermute(theirs, "core", CORES)
    low = jnp.where(core == 0, mine, came)
    high = jnp.where(core == 0, came, mine)
    pieces = jnp.concatenate([low, high], axis=0).reshape(NR, 24, LANES)
    pieces = lax.all_to_all(pieces, XZ, 0, 0, tiled=True)

    return pl.pallas_call(
        finish_kernel,
        out_shape=jax.ShapeDtypeStruct(momentum.shape, jnp.float32),
        compiler_params=pltpu.CompilerParams(vmem_limit_bytes=4 << 20),
        name="finish",
    )(pieces, momentum)


def solution(mesh):
    devices = mesh.devices.reshape(4, 8, 8, 2)
    fine = Mesh(devices, ("x", "z", "y", "core"))
    dp, hidden = ("x", "z"), ("y", "core")

    return jax.shard_map(
        local,
        mesh=fine,
        in_specs=(P(dp + hidden, None), P(dp, hidden), P(dp, hidden)),
        out_specs=P(dp, hidden),
        check_vma=False,
    )
```

```python
import jax
import jax.numpy as jnp
from jax import lax
from jax.experimental import pallas as pl
from jax.experimental.pallas import tpu as pltpu
from jax.sharding import Mesh, PartitionSpec as P


EPSILON = 1e-06
DECAY = 0.9
NR = 32
TOK = 128
LANES = 128
XZ = ("x", "z")
CORES = [(0, 1), (1, 0)]
PIECES = ((0, 56), (56, 48))


def gram_kernel(cols_ref, *refs):
    act_refs, outs, (gram_ref, g_ref, q_ref, sem) = refs[:-6], refs[-6:-4], refs[-4:]
    groups = cols_ref.shape[1] // 8
    depth = act_refs[0].shape[-1]
    lane_blocks = depth // LANES
    unroll = 26
    assert groups % unroll == 0

    def one(r, carry):
        act = jnp.concatenate([ref[r] for ref in act_refs], axis=0)
        g_ref[r] = jnp.dot(cols_ref[r], act, preferred_element_type=jnp.float32)
        return carry

    lax.fori_loop(0, NR, one, 0, unroll=NR)
    saves = []
    for part, out in enumerate(outs):
        rows = pl.ds(part * out.shape[1], out.shape[1])
        saves.append(pltpu.make_async_copy(g_ref.at[:, rows], out, sem.at[part]))
        saves[-1].start()
    q_ref[...] = jnp.zeros_like(q_ref)

    def pair_block(rb, sb, same):
        pairs = [(i, j) for i in range(4) for j in range(4) if not same or i <= j]

        def body(f, acc):
            acc = list(acc)
            for h in range(unroll):
                row = pl.multiple_of((f * unroll + h) * 8, 8)
                for lb in range(lane_blocks):
                    lanes = slice(lb * LANES, (lb + 1) * LANES)
                    left = [g_ref[rb * 4 + i, pl.ds(row, 8), lanes] for i in range(4)]
                    right = left
                    if not same:
                        right = [g_ref[sb * 4 + i, pl.ds(row, 8), lanes] for i in range(4)]
                    for n, (i, j) in enumerate(pairs):
                        acc[n] = acc[n] + left[i] * right[j]
            return tuple(acc)

        zero = jnp.zeros((8, LANES), jnp.float32)
        acc = lax.fori_loop(0, groups // unroll, body, (zero,) * len(pairs))
        for n, (i, j) in enumerate(pairs):
            left_id = rb * 4 + i
            base = lax.rem(left_id, 8) * 128 + lax.div(left_id, 8) * 32
            q_ref[pl.ds(base + sb * 4 + j, 1), :] = jnp.sum(acc[n], axis=0, keepdims=True)

    def outer(rb, carry):
        pair_block(rb, rb, True)

        def inner(sb, c):
            pair_block(rb, sb, False)
            return c

        return lax.fori_loop(rb + 1, NR // 4, inner, carry)

    lax.fori_loop(0, NR // 4, outer, 0)
    sums = lax.dot_general(
        jnp.ones((8, LANES), jnp.float32),
        q_ref[...],
        (((1,), (1,)), ((), ())),
        precision=lax.Precision.HIGHEST,
        preferred_element_type=jnp.float32,
    )
    for i in range(8):
        row = sums[i : i + 1, i * LANES : (i + 1) * LANES]
        for k in range(gram_ref.shape[0]):
            gram_ref[k, i : i + 1, :] = row
    for save in saves:
        save.wait()


def tree_weights(packed):
    gram = jnp.concatenate([packed[:, 32 * q : 32 * q + 32] for q in range(4)], axis=0)
    rows = lax.broadcasted_iota(jnp.int32, (NR, NR), 0)
    cols = lax.broadcasted_iota(jnp.int32, (NR, NR), 1)
    upper = jnp.where(rows < cols, gram, 0.0)
    quad = jnp.where(rows == cols, gram, 2.0 * upper)
    w_col = jnp.ones((NR, 1), jnp.float32)
    w_row = jnp.ones((1, NR), jnp.float32)
    for level in range(5):
        scale = w_col * w_row
        same_half = (rows >> level) == (cols >> level)
        same_pair = (rows >> (level + 1)) == (cols >> (level + 1))
        squares = jnp.where(same_half, quad * scale, 0.0)
        crosses = jnp.where(same_pair & (~same_half), upper * scale, 0.0)

        def both(values, mask):
            down = jnp.sum(values, axis=1, keepdims=True)
            across = jnp.sum(values, axis=0, keepdims=True)
            as_row = jnp.sum(jnp.where(mask, down, 0.0), axis=0, keepdims=True)
            as_col = jnp.sum(jnp.where(mask, across, 0.0), axis=1, keepdims=True)
            return as_col, as_row

        sq_col, sq_row = both(squares, same_half)
        cr_col, cr_row = both(crosses, same_pair)
        w_col = w_col * (1.0 - cr_col / (2.0 * (sq_col + EPSILON)))
        w_row = w_row * (1.0 - cr_row / (2.0 * (sq_row + EPSILON)))
    return w_col


def combine_kernel(core_ref, part_ref, own_ref, came_ref, out_ref, w_ref, ct_ref, g_ref, sem):
    core = core_ref[0]
    share = own_ref.shape[1]
    lane_blocks = own_ref.shape[2] // LANES
    loads = []
    for part, ref in enumerate((own_ref, came_ref)):
        for k, (start, size) in enumerate(PIECES):
            rows = pl.ds(start, size)
            loads.append(
                pltpu.make_async_copy(
                    ref.at[:, rows], g_ref.at[part, :, rows], sem.at[part * len(PIECES) + k]
                )
            )
            loads[-1].start()
    weights = tree_weights(jnp.sum(part_ref[...], axis=0))
    for r in range(NR):
        w_ref[r] = jnp.broadcast_to(weights[r : r + 1, :], (8, LANES))

    def add_up(part, f):
        row = pl.multiple_of(f * 8, 8)
        acc = [None] * lane_blocks
        for r in range(NR):
            weight = w_ref[r]
            for k in range(lane_blocks):
                term = g_ref[part, r, pl.ds(row, 8), k * LANES : (k + 1) * LANES] * weight
                acc[k] = term if r == 0 else acc[k] + term
        for k in range(lane_blocks):
            ct_ref[part, pl.ds(row, 8), k * LANES : (k + 1) * LANES] = acc[k]

    for part in range(2):
        tail = ct_ref.shape[1] - share
        ct_ref[part, pl.ds(share, tail), :] = jnp.zeros((tail, ct_ref.shape[2]), jnp.float32)
        for k, (start, size) in enumerate(PIECES):
            loads[part * len(PIECES) + k].wait()

            def body(f, carry):
                add_up(part, f)
                return carry

            lax.fori_loop(start // 8, (start + size) // 8, body, 0)
        place = core if part == 0 else 1 - core
        for k in range(lane_blocks):
            lanes = slice(k * LANES, (k + 1) * LANES)
            out_ref[place, lanes, :] = ct_ref[part, :, lanes].T


def finish_kernel(pieces_ref, momentum_ref, out_ref):
    width = momentum_ref.shape[1] // pieces_ref.shape[0]
    row = jnp.concatenate([pieces_ref[k][:, :width] for k in range(pieces_ref.shape[0])], axis=1)
    out_ref[...] = DECAY * momentum_ref[...] + row


def ring(block):
    size = lax.axis_size("y")
    up = [(i, (i + 1) % size) for i in range(size)]
    down = [(i, (i - 1) % size) for i in range(size)]
    above, below = [block], [block]
    for step in range(size // 2):
        below.append(lax.ppermute(below[-1], "y", up))
        if step < size // 2 - 1:
            above.append(lax.ppermute(above[-1], "y", down))
    return above + below[:0:-1]


def local(activations, grad_out, momentum):
    core = lax.axis_index("core")
    columns = grad_out.shape[1]
    share = columns // NR
    depth = activations.shape[1] // 2

    halves = activations.reshape(8, 2, depth).transpose(1, 0, 2)
    halves = jnp.broadcast_to(halves[None], (NR, 2, 8, depth)).reshape(2 * NR, 8, depth)
    halves = lax.all_to_all(halves, ("x", "z", "core"), 0, 0, tiled=True)
    halves = halves.reshape(NR * 16, depth)

    shift = 16 * lax.axis_index("y")
    rolled = lax.dynamic_slice_in_dim(jnp.concatenate([grad_out, grad_out], axis=0), shift, TOK, 0)
    acts = ring(halves.reshape(NR, 16, depth))
    own = lax.all_to_all(rolled.T.reshape(NR, share, TOK), XZ, 0, 0, tiled=True)
    other = lax.ppermute(own, "core", CORES)
    cols = jnp.concatenate([own, other], axis=1)

    grads, to_swap, gram = pl.pallas_call(
        gram_kernel,
        out_shape=[
            jax.ShapeDtypeStruct((NR, share, depth), jnp.float32),
            jax.ShapeDtypeStruct((NR, share, depth), jnp.float32),
            jax.ShapeDtypeStruct((16, 8, LANES), jnp.float32),
        ],
        out_specs=[
            pl.BlockSpec(memory_space=pltpu.HBM),
            pl.BlockSpec(memory_space=pltpu.HBM),
            pl.BlockSpec(memory_space=pltpu.VMEM),
        ],
        scratch_shapes=[
            pltpu.VMEM((NR, 2 * share, depth), jnp.float32),
            pltpu.VMEM((1024, LANES), jnp.float32),
            pltpu.SemaphoreType.DMA((2,)),
        ],
        compiler_params=pltpu.CompilerParams(vmem_limit_bytes=48 << 20),
        name="gram",
    )(cols, *acts)

    gram = lax.all_to_all(gram, ("z", "core"), 0, 0, tiled=True)
    came = lax.ppermute(to_swap, "core", CORES)
    gram = jnp.sum(gram, axis=0)
    gram = lax.all_to_all(jnp.broadcast_to(gram, (32, 8, LANES)), ("x", "y"), 0, 0, tiled=True)

    pieces = pl.pallas_call(
        combine_kernel,
        out_shape=jax.ShapeDtypeStruct((2, depth, LANES), jnp.float32),
        scratch_shapes=[
            pltpu.VMEM((NR, 8, LANES), jnp.float32),
            pltpu.VMEM((2, LANES, depth), jnp.float32),
            pltpu.VMEM((2, NR, share, depth), jnp.float32),
            pltpu.SemaphoreType.DMA((2 * len(PIECES),)),
        ],
        in_specs=[
            pl.BlockSpec(memory_space=pltpu.SMEM),
            pl.BlockSpec(memory_space=pltpu.VMEM),
            pl.BlockSpec(memory_space=pltpu.HBM),
            pl.BlockSpec(memory_space=pltpu.HBM),
        ],
        compiler_params=pltpu.CompilerParams(vmem_limit_bytes=52 << 20),
        name="combine",
    )(core.astype(jnp.int32).reshape(1), gram, grads, came)
    pieces = pieces.reshape(NR, 24, LANES)
    pieces = lax.all_to_all(pieces, XZ, 0, 0, tiled=True)

    return pl.pallas_call(
        finish_kernel,
        out_shape=jax.ShapeDtypeStruct(momentum.shape, jnp.float32),
        compiler_params=pltpu.CompilerParams(vmem_limit_bytes=4 << 20),
        name="finish",
    )(pieces, momentum)


def solution(mesh):
    devices = mesh.devices.reshape(4, 8, 8, 2)
    fine = Mesh(devices, ("x", "z", "y", "core"))
    dp, hidden = ("x", "z"), ("y", "core")

    return jax.shard_map(
        local,
        mesh=fine,
        in_specs=(P(dp + hidden, None), P(dp, hidden), P(dp, hidden)),
        out_specs=P(dp, hidden),
        check_vma=False,
    )
```

```python
import functools

import jax
import jax.numpy as jnp
from jax import lax
from jax.experimental import pallas as pl
from jax.experimental.pallas import tpu as pltpu
from jax.sharding import Mesh, PartitionSpec as P


EPSILON = 1e-06
DECAY = 0.9
NR = 32
GRANTS = (48, 48)
TOK = 128
LANES = 128
XZ = ("x", "z")
CORES = [(0, 1), (1, 0)]
CHUNKS = ((0, 128), (128, 256))
PIECES = ((0, 56), (56, 48))


def gram_kernel(start, n_before, cols_ref, *refs):
    before, refs = refs[2 * n_before : n_before * 3], refs[3 * n_before :]
    act_refs, outs, (gram_ref, g_ref, q_ref, sem) = refs[:-6], refs[-6:-4], refs[-4:]
    groups = cols_ref.shape[1] // 8
    depth = g_ref.shape[-1]
    lane_blocks = depth // LANES
    unroll = 26
    assert groups % unroll == 0
    opposite = len(act_refs) // 2

    for r in range(NR):
        rows = [
            ref[r] if k == opposite else ref[r, :, start : start + depth]
            for k, ref in enumerate(act_refs)
        ]
        act = jnp.concatenate(rows, axis=0)
        g_ref[r] = jnp.dot(cols_ref[r], act, preferred_element_type=jnp.float32)

    saves = []
    for part, out in enumerate(outs):
        rows = pl.ds(part * out.shape[1], out.shape[1])
        place = out.at[:, :, pl.ds(start, depth)]
        saves.append(pltpu.make_async_copy(g_ref.at[:, rows], place, sem.at[part]))
        saves[-1].start()
    q_ref[...] = jnp.zeros_like(q_ref)

    def pair_block(rb, sb, same):
        pairs = [(i, j) for i in range(4) for j in range(4) if not same or i <= j]

        def body(f, acc):
            acc = list(acc)
            for h in range(unroll):
                row = pl.multiple_of((f * unroll + h) * 8, 8)
                for lb in range(lane_blocks):
                    lanes = slice(lb * LANES, (lb + 1) * LANES)
                    left = [g_ref[rb * 4 + i, pl.ds(row, 8), lanes] for i in range(4)]
                    right = left
                    if not same:
                        right = [g_ref[sb * 4 + i, pl.ds(row, 8), lanes] for i in range(4)]
                    for n, (i, j) in enumerate(pairs):
                        acc[n] = acc[n] + left[i] * right[j]
            return tuple(acc)

        zero = jnp.zeros((8, LANES), jnp.float32)
        acc = lax.fori_loop(0, groups // unroll, body, (zero,) * len(pairs))
        for n, (i, j) in enumerate(pairs):
            left_id = rb * 4 + i
            base = lax.rem(left_id, 8) * 128 + lax.div(left_id, 8) * 32
            q_ref[pl.ds(base + sb * 4 + j, 1), :] = jnp.sum(acc[n], axis=0, keepdims=True)

    def outer(rb, carry):
        pair_block(rb, rb, True)

        def inner(sb, c):
            pair_block(rb, sb, False)
            return c

        return lax.fori_loop(rb + 1, NR // 4, inner, carry)

    lax.fori_loop(0, NR // 4, outer, 0)
    sums = lax.dot_general(
        jnp.ones((8, LANES), jnp.float32),
        q_ref[...],
        (((1,), (1,)), ((), ())),
        precision=lax.Precision.HIGHEST,
        preferred_element_type=jnp.float32,
    )
    for i in range(8):
        row = sums[i : i + 1, i * LANES : (i + 1) * LANES]
        for ref in before:
            row = row + ref[0, i : i + 1, :]
        for k in range(gram_ref.shape[0]):
            gram_ref[k, i : i + 1, :] = row
    for save in saves:
        save.wait()


def tree_weights(packed):
    gram = jnp.concatenate([packed[:, 32 * q : 32 * q + 32] for q in range(4)], axis=0)
    rows = lax.broadcasted_iota(jnp.int32, (NR, NR), 0)
    cols = lax.broadcasted_iota(jnp.int32, (NR, NR), 1)
    upper = jnp.where(rows < cols, gram, 0.0)
    quad = jnp.where(rows == cols, gram, 2.0 * upper)
    w_col = jnp.ones((NR, 1), jnp.float32)
    w_row = jnp.ones((1, NR), jnp.float32)
    for level in range(5):
        scale = w_col * w_row
        same_half = (rows >> level) == (cols >> level)
        same_pair = (rows >> (level + 1)) == (cols >> (level + 1))
        squares = jnp.where(same_half, quad * scale, 0.0)
        crosses = jnp.where(same_pair & (~same_half), upper * scale, 0.0)

        def both(values, mask):
            down = jnp.sum(values, axis=1, keepdims=True)
            across = jnp.sum(values, axis=0, keepdims=True)
            as_row = jnp.sum(jnp.where(mask, down, 0.0), axis=0, keepdims=True)
            as_col = jnp.sum(jnp.where(mask, across, 0.0), axis=1, keepdims=True)
            return as_col, as_row

        sq_col, sq_row = both(squares, same_half)
        cr_col, cr_row = both(crosses, same_pair)
        w_col = w_col * (1.0 - cr_col / (2.0 * (sq_col + EPSILON)))
        w_row = w_row * (1.0 - cr_row / (2.0 * (sq_row + EPSILON)))
    return w_col


def combine_kernel(core_ref, part_ref, own_ref, came_ref, out_ref, w_ref, ct_ref, g_ref, sem):
    core = core_ref[0]
    share = own_ref.shape[1]
    lane_blocks = own_ref.shape[2] // LANES
    loads = []
    for part, ref in enumerate((own_ref, came_ref)):
        for k, (start, size) in enumerate(PIECES):
            rows = pl.ds(start, size)
            loads.append(
                pltpu.make_async_copy(
                    ref.at[:, rows], g_ref.at[part, :, rows], sem.at[part * len(PIECES) + k]
                )
            )
            loads[-1].start()
    weights = tree_weights(jnp.sum(part_ref[...], axis=0))
    for r in range(NR):
        w_ref[r] = jnp.broadcast_to(weights[r : r + 1, :], (8, LANES))

    def add_up(part, f):
        row = pl.multiple_of(f * 8, 8)
        acc = [None] * lane_blocks
        for r in range(NR):
            weight = w_ref[r]
            for k in range(lane_blocks):
                term = g_ref[part, r, pl.ds(row, 8), k * LANES : (k + 1) * LANES] * weight
                acc[k] = term if r == 0 else acc[k] + term
        for k in range(lane_blocks):
            ct_ref[part, pl.ds(row, 8), k * LANES : (k + 1) * LANES] = acc[k]

    for part in range(2):
        tail = ct_ref.shape[1] - share
        ct_ref[part, pl.ds(share, tail), :] = jnp.zeros((tail, ct_ref.shape[2]), jnp.float32)
        for k, (start, size) in enumerate(PIECES):
            loads[part * len(PIECES) + k].wait()

            def body(f, carry):
                add_up(part, f)
                return carry

            lax.fori_loop(start // 8, (start + size) // 8, body, 0)
        place = core if part == 0 else 1 - core
        for k in range(lane_blocks):
            lanes = slice(k * LANES, (k + 1) * LANES)
            out_ref[place, lanes, :] = ct_ref[part, :, lanes].T


def finish_kernel(pieces_ref, momentum_ref, out_ref):
    width = momentum_ref.shape[1] // pieces_ref.shape[0]
    row = jnp.concatenate([pieces_ref[k][:, :width] for k in range(pieces_ref.shape[0])], axis=1)
    out_ref[...] = DECAY * momentum_ref[...] + row


def ring(block):
    size = lax.axis_size("y")
    up = [(i, (i + 1) % size) for i in range(size)]
    down = [(i, (i - 1) % size) for i in range(size)]
    above, below = [block], [block]
    for _ in range(size // 2 - 1):
        below.append(lax.ppermute(below[-1], "y", up))
        above.append(lax.ppermute(above[-1], "y", down))
    opposite = []
    for start, width in CHUNKS:
        part = below[-1][:, :, start : start + width]
        opposite.append(lax.ppermute(part, "y", up))
    return above, opposite, below[:0:-1]


def local(activations, grad_out, momentum):
    core = lax.axis_index("core")
    columns = grad_out.shape[1]
    share = columns // NR
    depth = activations.shape[1] // 2

    halves = activations.reshape(8, 2, depth).transpose(1, 0, 2)
    halves = jnp.broadcast_to(halves[None], (NR, 2, 8, depth)).reshape(2 * NR, 8, depth)
    halves = lax.all_to_all(halves, ("x", "z", "core"), 0, 0, tiled=True)
    halves = halves.reshape(NR * 16, depth)

    shift = 16 * lax.axis_index("y")
    rolled = lax.dynamic_slice_in_dim(jnp.concatenate([grad_out, grad_out], axis=0), shift, TOK, 0)
    above, opposite, below = ring(halves.reshape(NR, 16, depth))
    own = lax.all_to_all(rolled.T.reshape(NR, share, TOK), XZ, 0, 0, tiled=True)
    other = lax.ppermute(own, "core", CORES)
    cols = jnp.concatenate([own, other], axis=1)

    carried = ()
    for k, (start, width) in enumerate(CHUNKS):
        carried = pl.pallas_call(
            functools.partial(gram_kernel, start, k),
            out_shape=[
                jax.ShapeDtypeStruct((NR, share, depth), jnp.float32),
                jax.ShapeDtypeStruct((NR, share, depth), jnp.float32),
                jax.ShapeDtypeStruct((16, 8, LANES), jnp.float32),
            ],
            in_specs=[pl.BlockSpec(memory_space=pltpu.VMEM)]
            + [pl.BlockSpec(memory_space=pltpu.HBM)] * (2 * k)
            + [pl.BlockSpec(memory_space=pltpu.VMEM)] * (8 + k),
            out_specs=[
                pl.BlockSpec(memory_space=pltpu.HBM),
                pl.BlockSpec(memory_space=pltpu.HBM),
                pl.BlockSpec(memory_space=pltpu.VMEM),
            ],
            scratch_shapes=[
                pltpu.VMEM((NR, 2 * share, width), jnp.float32),
                pltpu.VMEM((1024, LANES), jnp.float32),
                pltpu.SemaphoreType.DMA((2,)),
            ],
            input_output_aliases={1: 0, 2: 1} if k else {},
            compiler_params=pltpu.CompilerParams(vmem_limit_bytes=GRANTS[k] << 20),
            name="gram",
        )(cols, *carried, *above, opposite[k], *below)
    grads, to_swap, gram = carried

    gram = lax.all_to_all(gram, ("z", "core"), 0, 0, tiled=True)
    came = lax.ppermute(to_swap, "core", CORES)
    gram = jnp.sum(gram, axis=0)
    gram = lax.all_to_all(jnp.broadcast_to(gram, (32, 8, LANES)), ("x", "y"), 0, 0, tiled=True)

    pieces = pl.pallas_call(
        combine_kernel,
        out_shape=jax.ShapeDtypeStruct((2, depth, LANES), jnp.float32),
        scratch_shapes=[
            pltpu.VMEM((NR, 8, LANES), jnp.float32),
            pltpu.VMEM((2, LANES, depth), jnp.float32),
            pltpu.VMEM((2, NR, share, depth), jnp.float32),
            pltpu.SemaphoreType.DMA((2 * len(PIECES),)),
        ],
        in_specs=[
            pl.BlockSpec(memory_space=pltpu.SMEM),
            pl.BlockSpec(memory_space=pltpu.VMEM),
            pl.BlockSpec(memory_space=pltpu.HBM),
            pl.BlockSpec(memory_space=pltpu.HBM),
        ],
        compiler_params=pltpu.CompilerParams(vmem_limit_bytes=52 << 20),
        name="combine",
    )(core.astype(jnp.int32).reshape(1), gram, grads, came)
    pieces = pieces.reshape(NR, 24, LANES)
    pieces = lax.all_to_all(pieces, XZ, 0, 0, tiled=True)

    return pl.pallas_call(
        finish_kernel,
        out_shape=jax.ShapeDtypeStruct(momentum.shape, jnp.float32),
        compiler_params=pltpu.CompilerParams(vmem_limit_bytes=4 << 20),
        name="finish",
    )(pieces, momentum)


def solution(mesh):
    devices = mesh.devices.reshape(4, 8, 8, 2)
    fine = Mesh(devices, ("x", "z", "y", "core"))
    dp, hidden = ("x", "z"), ("y", "core")

    return jax.shard_map(
        local,
        mesh=fine,
        in_specs=(P(dp + hidden, None), P(dp, hidden), P(dp, hidden)),
        out_specs=P(dp, hidden),
        check_vma=False,
    )
```
